32 devices in a mesh: seq: 8 (over z, x), head: 4 (over y, core).
Axes of the slice: x: 2, y: 2, z: 4, core: 2. Of those that a mesh axis runs over, the one named last changes fastest.
Arguments:
- tokens: bfloat16 [2, 2048, 2048], P(None, 'seq'), may hold values from -6 to 6
- w_query: bfloat16 [2048, 2048], P('seq', 'head'), may hold values from -0.125 to 0.125
- w_key: bfloat16 [2048, 2048], P('seq', 'head'), may hold values from -0.125 to 0.125
- w_value: bfloat16 [2048, 2048], P('seq', 'head'), may hold values from -0.125 to 0.125
- w_gate: bfloat16 [2048, 2048], P('seq', 'head'), may hold values from -0.125 to 0.125
- w_out: bfloat16 [2048, 2048], P('head', 'seq'), may hold values from -0.125 to 0.125
- w_first: bfloat16 [2048, 5632], P('seq', 'head'), may hold values from -0.125 to 0.125
- w_second: bfloat16 [2048, 5632], P('seq', 'head'), may hold values from -0.125 to 0.125
- w_down: bfloat16 [5632, 2048], P('head', 'seq'), may hold values from -0.078125 to 0.078125
- decay_rate: float32 [16], P('head'), may hold values from 7.6293945e-06 to 0.03125
- out_grad: bfloat16 [2, 2048, 2048], P(None, 'seq'), may hold values from -6 to 6
Outputs:
- layer_out: bfloat16 [2, 2048, 2048], P(None, 'seq')
- input_grad: float32 [2, 2048, 2048], P(None, 'seq')
- grad_query: float32 [2048, 2048], P('seq', 'head')
- grad_key: float32 [2048, 2048], P('seq', 'head')
- grad_value: float32 [2048, 2048], P('seq', 'head')
- grad_gate: float32 [2048, 2048], P('seq', 'head')
- grad_out: float32 [2048, 2048], P('head', 'seq')
- grad_first: float32 [2048, 5632], P('seq', 'head')
- grad_second: float32 [2048, 5632], P('seq', 'head')
- grad_down: float32 [5632, 2048], P('head', 'seq')
The draws below stay inside these ranges and needn't reach their ends.
All inputs are finite; a program needn't handle non-finite values.
Results may differ from the reference program's by a relative error of at most 0.018.
Values may be sent and summed in bfloat16 or wider, within the bound.
No kernel may reach another device: no remote copies, remote signals or barrier semaphores. Data moves between devices by JAX's collectives and lax.ppermute only.
A program may use at most 256 MiB of HBM per device.

```python
import math
from functools import partial
import jax
import jax.numpy as jnp
from jax import lax

D = 2048
HEADS = 16
HEAD_DIM = 128
FF = 5632
BLOCK = 256
MICRO = 2
LENGTH = 2048


def block_scale(rng, extent, cuts, least, high):
    loudness = 1.0
    for axis_at, blocks in cuts:
        heights = jax.random.uniform(jax.random.fold_in(jax.random.fold_in(rng, 6), axis_at), (blocks,), jnp.float32, least / len(cuts), high / len(cuts))
        loudness = loudness * jnp.repeat(jnp.exp(heights), extent[axis_at] // blocks).reshape((-1,) + (1,) * (len(extent) - 1 - axis_at))
    return loudness


def centred(rng, shape, deviation, bound, shards=(), held_as=jnp.bfloat16):
    factor_of = block_scale(rng, shape, shards, -0.22, 0.18) if shards else 1.0
    values = jax.random.normal(rng, shape, jnp.float32) * deviation * factor_of
    return jnp.minimum(jnp.maximum(values, -bound), bound).astype(held_as)


def setup_inputs(seed: int = 0) -> dict:
    streams_of = jax.random.split(jax.random.key(seed), 12)
    return {
        "tokens": centred(streams_of[0], (MICRO, LENGTH, D), 1.0, 6.0, ((1, 8),)),
        "w_query": centred(streams_of[1], (D, D), D ** -0.5, 0.125, ((0, 8), (1, 4))),
        "w_key": centred(streams_of[2], (D, D), D ** -0.5, 0.125, ((0, 8), (1, 4))),
        "w_value": centred(streams_of[3], (D, D), D ** -0.5, 0.125, ((0, 8), (1, 4))),
        "w_gate": centred(streams_of[4], (D, D), D ** -0.5, 0.125, ((0, 8), (1, 4))),
        "w_out": centred(streams_of[5], (D, D), D ** -0.5, 0.125, ((0, 4), (1, 8))),
        "w_first": centred(streams_of[6], (D, FF), D ** -0.5, 0.125, ((0, 8), (1, 4))),
        "w_second": centred(streams_of[7], (D, FF), D ** -0.5, 0.125, ((0, 8), (1, 4))),
        "w_down": centred(streams_of[8], (FF, D), FF ** -0.5, 0.078125, ((0, 4), (1, 8))),
        "decay_rate": jnp.clip(jnp.exp(math.log(0.03125) - 8.317766 * jax.random.uniform(streams_of[9], (HEADS,), jnp.float32) ** block_scale(streams_of[9], (HEADS,), ((0, 4),), -0.2, 0.2)), 7.62939453125e-06, 0.03125),
        "out_grad": centred(streams_of[10], (MICRO, LENGTH, D), 1.0, 6.0, ((1, 8),)),
    }


EPSILON = 1e-06
HIGHEST = lax.Precision.HIGHEST

@jax.custom_vjp
def low(v):
    return lax.optimization_barrier(v.astype(jnp.bfloat16)).astype(jnp.float32)

@jax.custom_vjp
def low_back(v):
    return v

def low_keep(v):
    return (low(v), None)

def low_pass(kept, grad):
    return (grad,)

def back_keep(v):
    return (v, None)

def back_low(kept, grad):
    return (low(grad),)
low.defvjp(low_keep, low_pass)
low_back.defvjp(back_keep, back_low)

def matmul_hi(left, right):
    return jnp.dot(left, right, precision=HIGHEST)

def srms(values):
    return values * lax.rsqrt(lax.optimization_barrier(jnp.mean(values * values, axis=-1, keepdims=True)) + EPSILON)

def attend_block(carry, pieces, rates):
    queries, keys_in, values_in = pieces
    block_len = queries.shape[0]
    positions = jnp.arange(block_len, dtype=jnp.float32)
    distance = positions[:, None] - positions[None, :]
    is_causal = distance >= 0
    decay_mask = jnp.where(is_causal[None], jnp.exp(-rates[:, None, None] * jnp.where(is_causal, distance, 0.0)[None]), 0.0)
    scores = low_back(jnp.einsum('thd,shd->hts', queries, keys_in, precision=HIGHEST))
    weights = low(scores * decay_mask)
    intra = jnp.einsum('hts,shd->thd', weights, values_in, precision=HIGHEST)
    lead_decay = jnp.exp(-rates[None, :] * (positions[:, None] + 1.0))
    tail_decay = jnp.exp(-rates[None, :] * (block_len - 1.0 - positions[:, None]))
    inter = jnp.einsum('thd,hde->the', queries * lead_decay[:, :, None], carry, precision=HIGHEST)
    local_state = jnp.einsum('shd,she->hde', keys_in * tail_decay[:, :, None], values_in, precision=HIGHEST)
    new_state = jnp.exp(-rates * block_len)[:, None, None] * carry + local_state
    return (new_state, intra + inter)

def layer(resid_in, w_query, w_key, w_value, w_gate, w_out, w_first, w_second, w_down, rates):
    normed_in = low(srms(resid_in))
    query_pre = low_back(matmul_hi(normed_in, w_query))
    key_pre = low_back(matmul_hi(normed_in, w_key))
    queries = low(jax.nn.silu(query_pre))
    keys_low = low(jax.nn.silu(key_pre))
    values_low = low(low_back(matmul_hi(normed_in, w_value)))
    gate_lin = low_back(matmul_hi(normed_in, w_gate))
    row_count = resid_in.shape[0]
    shape = (row_count // BLOCK, BLOCK, HEADS, HEAD_DIM)
    block_step = jax.checkpoint(partial(attend_block, rates=rates))
    start_state = jnp.zeros((HEADS, HEAD_DIM, HEAD_DIM), jnp.float32)
    _, blocks_out = lax.scan(block_step, start_state, (queries.reshape(shape), keys_low.reshape(shape), values_low.reshape(shape)))
    attn_raw = low_back(blocks_out.reshape(row_count, HEADS * HEAD_DIM))
    gated = low(srms(attn_raw) * gate_lin)
    resid_mid = resid_in + low_back(matmul_hi(gated, w_out))
    normed_mid = low(srms(resid_mid))
    first_pre = low_back(matmul_hi(normed_mid, w_first))
    second_pre = low_back(matmul_hi(normed_mid, w_second))
    product = low(first_pre * second_pre)
    return resid_mid + matmul_hi(product, w_down)

def reference(tokens, w_query, w_key, w_value, w_gate, w_out, w_first, w_second, w_down, decay_rate, out_grad):
    matrices = tuple((matrix.astype(jnp.float32) for matrix in (w_query, w_key, w_value, w_gate, w_out, w_first, w_second, w_down)))

    def run_sequence(grad_total, pair):
        resid_in, upstream = pair
        result, pullback = jax.vjp(lambda resid, *mats: layer(resid, *mats, decay_rate), resid_in.astype(jnp.float32), *matrices)
        grads = pullback(upstream.astype(jnp.float32))
        grad_total = tuple((total + grad for total, grad in zip(grad_total, grads[1:])))
        return (grad_total, (result.astype(jnp.bfloat16), grads[0]))
    zero_total = tuple((jnp.zeros_like(matrix) for matrix in matrices))
    grad_total, (outputs, input_grads) = lax.scan(run_sequence, zero_total, (tokens, out_grad))
    return (outputs, input_grads, grad_total[0], grad_total[1], grad_total[2], grad_total[3], grad_total[4], grad_total[5], grad_total[6], grad_total[7])
```

```python
import jax
import jax.numpy as jnp
from jax import lax
from jax.sharding import Mesh
from jax.sharding import PartitionSpec as P

EPSILON = 1e-06
BF16 = jnp.bfloat16
F32 = jnp.float32
PLANE = 2
SWAP = [(0, 1), (1, 0)]


def dot_nn(left, right):
    return jnp.dot(left, right, preferred_element_type=F32)


def dot_tn(left, right):
    return lax.dot_general(left, right, (((0,), (0,)), ((), ())), preferred_element_type=F32)


def dot_nt(left, right):
    return lax.dot_general(left, right, (((1,), (1,)), ((), ())), preferred_element_type=F32)


def after(value, *earlier):
    return lax.optimization_barrier((value, earlier))[0]


def swap_u(value):
    return lax.ppermute(value, "u", SWAP)


def swap_h(value, bit):
    count = lax.axis_size("head")
    return lax.ppermute(value, "head", [(i, i ^ bit) for i in range(count)])


def shift_t(value, by):
    count = lax.axis_size("t")
    return lax.ppermute(
        value, "t", [(i, i + by) for i in range(count) if 0 <= i + by < count]
    )


def is_line():
    return lax.axis_size("t") <= 4


def shift_of():
    return lax.axis_index("t") if is_line() else jnp.int32(0)


def rotate(values, back=False):
    count = lax.axis_size("t")
    if not is_line():
        return values
    width = values.shape[-1] // count
    start = shift_of()
    start = (count - start) if back else start
    blocks = [
        lax.dynamic_slice_in_dim(
            values, ((start + r) % count) * width, width, axis=values.ndim - 1
        )
        for r in range(count)
    ]
    return jnp.concatenate(blocks, axis=-1)


def gather_t(pieces):
    count = lax.axis_size("t")
    if not is_line():
        whole = lax.all_gather(pieces, "t")
        return [whole[r] for r in range(count)], pieces
    mine = lax.axis_index("t")
    up, down = pieces, pieces
    ups, downs = [], []
    for step in range(1, count):
        up = lax.ppermute(up, "t", [(i, i + 1) for i in range(step - 1, count - 1)])
        down = lax.ppermute(down, "t", [(i + 1, i) for i in range(0, count - step)])
        ups.append(up)
        downs.append(down)
    slots = [pieces]
    for r in range(1, count):
        slots.append(jnp.where(mine + r < count, downs[r - 1], ups[count - r - 1]))
    return slots, (up, down)


def scatter_t(slots):
    count = lax.axis_size("t")
    if not is_line():
        whole = jnp.stack([slot.astype(BF16) for slot in slots])
        return lax.psum_scatter(whole, "t", scatter_dimension=0, tiled=False).astype(F32)
    up = slots[count - 1].astype(BF16)
    down = slots[1].astype(BF16)
    for step in range(count - 1, 0, -1):
        up = lax.ppermute(up, "t", [(i, i + 1) for i in range(0, count - step)])
        down = lax.ppermute(down, "t", [(i + 1, i) for i in range(step - 1, count - 1)])
        if step > 1:
            up = (up.astype(F32) + slots[step - 1]).astype(BF16)
            down = (down.astype(F32) + slots[count - step + 1]).astype(BF16)
    return slots[0].astype(F32) + up.astype(F32) + down.astype(F32)


def plane_reduce(partial):
    rows, width = partial.shape
    parts = partial.reshape(2, 2, 2, rows // 8, width)
    total = parts[:, :, 0].astype(F32) + swap_h(parts[:, :, 1].astype(BF16), 1).astype(F32)
    half = width // 2
    left, right = total[..., :half], total[..., half:]
    left = left[:, 0] + swap_u(left[:, 1].astype(BF16)).astype(F32)
    right = right[0] + swap_h(right[1].astype(BF16), 2).astype(F32)
    left = left[0] + swap_h(left[1].astype(BF16), 2).astype(F32)
    right = right[0] + swap_u(right[1].astype(BF16)).astype(F32)
    return jnp.concatenate([left, right], axis=-1)


def plane_reduce_small(values):
    parts = values.reshape(2, 2, 2, -1)
    total = parts[:, :, 0] + swap_h(parts[:, :, 1], 1)
    total = total[:, 0] + swap_u(total[:, 1])
    return total[0] + swap_h(total[1], 2)


def plane_gather(own):
    rows, width = own.shape
    half = width // 2
    left, right = own[:, :half], own[:, half:]
    left = jnp.stack([left, swap_h(left, 2)])
    right = jnp.stack([right, swap_u(right)])
    left = jnp.stack([left, swap_u(left)], axis=1)
    right = jnp.stack([right, swap_h(right, 2)], axis=0)
    both = jnp.concatenate([left, right], axis=-1)
    both = jnp.stack([both, swap_h(both, 1)], axis=2)
    return both.reshape(8 * rows, width)


def plane_gather_small(own):
    both = jnp.stack([own, swap_h(own, 2)])
    both = jnp.stack([both, swap_u(both)], axis=1)
    both = jnp.stack([both, swap_h(both, 1)], axis=2)
    return both


def head_gather(own):
    both = jnp.stack([own, swap_h(own, 2)])
    return jnp.stack([both, swap_h(both, 1)], axis=1)


def own_first(values, back=False):
    place = lax.axis_index("head")
    low, high = place & 1, place >> 1
    if not back:
        values = values.reshape(2, 2, values.shape[1] // 2, values.shape[2])
    values = jnp.where(high == 1, values[::-1], values)
    values = jnp.where(low == 1, values[:, ::-1], values)
    if back:
        values = values.reshape(2, 2 * values.shape[2], values.shape[3])
    return values


def from_partner(values):
    part = swap_u(values[0, 0])
    part = jnp.stack([part, swap_h(part, 1)])
    return jnp.stack([part, swap_h(part, 2)])


def pair_rows(mine, other):
    both = jnp.stack([mine, other], axis=1)
    return both.reshape(-1, both.shape[-1])


def halves(values, axis):
    size = values.shape[axis] // 2
    mine = lax.axis_index("u")
    return (
        lax.dynamic_slice_in_dim(values, mine * size, size, axis=axis),
        lax.dynamic_slice_in_dim(values, (1 - mine) * size, size, axis=axis),
    )


def in_u_order(mine, other, axis):
    first = lax.axis_index("u") == 0
    return jnp.concatenate(
        [jnp.where(first, mine, other), jnp.where(first, other, mine)], axis=axis
    )


def share_u(values, split, join):
    mine, theirs = halves(values, split)
    return in_u_order(mine, swap_u(theirs), join)


def rms_scale(values):
    return lax.rsqrt(jnp.mean(values * values, axis=-1, keepdims=True) + EPSILON)


def rms_back(values, scale, upstream):
    inner = jnp.sum(upstream * values, axis=-1, keepdims=True)
    return scale * upstream - scale * scale * scale / values.shape[-1] * values * inner


def silu_slope(values):
    sigma = jax.nn.sigmoid(values)
    return sigma * (1.0 + values * (1.0 - sigma))


def earlier_state(local_state, decay, reverse):
    count = lax.axis_size("t")
    sign = -1 if reverse else 1
    low = local_state.astype(BF16)
    if is_line():
        total = shift_t(low, sign).astype(F32)
        weight = decay
        for by in range(2, count):
            total = total + weight * shift_t(low, sign * by).astype(F32)
            weight = weight * decay
        return total
    total = shift_t(local_state, sign)
    by, weight = 1, decay
    while by < count:
        total = total + weight * shift_t(total, sign * by)
        by, weight = by * 2, weight * weight
    return total


def local(
    tokens, w_query, w_key, w_value, w_gate, w_out, w_first, w_second, w_down, decay_rate, out_grad
):
    batch, piece, width = tokens.shape
    u_index = lax.axis_index("u")
    place = lax.axis_index("head")
    count = lax.axis_size("t")
    hidden = w_first.shape[1] // PLANE
    lanes = w_query.shape[1] // PLANE
    head_dim = lanes * PLANE // decay_rate.shape[0]
    heads = lanes // head_dim
    length = piece * PLANE
    rows = batch * length

    def columns(*matrices):
        mine, theirs = zip(*(halves(m, 1) for m in matrices))
        return in_u_order(
            jnp.concatenate(mine, axis=1), swap_u(jnp.concatenate(theirs, axis=1)), 0
        )

    piece_qk = columns(w_query, w_key)
    piece_vg = columns(w_value, w_gate)
    piece_out = share_u(w_out, 0, 1)
    piece_first = share_u(w_first.T, 0, 1)
    piece_second = share_u(w_second.T, 0, 1)
    piece_down = share_u(w_down, 0, 1)
    slots_qk, end_qk = gather_t(piece_qk)
    slots_vg, end_vg = gather_t(piece_vg)
    slots_out, end_out = gather_t(after(piece_out, end_qk))
    slots_first, end_first = gather_t(after(piece_first, end_vg))
    slots_second, end_second = gather_t(after(piece_second, end_out))
    slots_down, _ = gather_t(after(piece_down, end_first))
    full_qk = jnp.concatenate(slots_qk, axis=0)
    full_vg = jnp.concatenate(slots_vg, axis=0)
    full_out = jnp.concatenate(slots_out, axis=1)
    full_first = jnp.concatenate(slots_first, axis=1)
    full_second = jnp.concatenate(slots_second, axis=1)
    full_down = jnp.concatenate(slots_down, axis=1)

    x_rows = rotate(own_first(tokens)).astype(F32)
    normed_mine = (x_rows * rms_scale(x_rows)).astype(BF16)
    normed_in = pair_rows(normed_mine, from_partner(normed_mine))
    x_own = x_rows[0, 0]
    scale_in = rms_scale(x_own)
    gy_mine = rotate(own_first(out_grad))
    gy = pair_rows(gy_mine, from_partner(gy_mine))
    gy_own = gy_mine[0, 0].astype(F32)

    rates = lax.dynamic_slice_in_dim(decay_rate, u_index * heads, heads)
    span = jnp.arange(piece // 2)
    order = jnp.arange(2)
    position = (
        (order[:, None, None] ^ u_index) * piece
        + (order[None, :, None] ^ (place & 1)) * (piece // 2)
        + span[None, None, :]
    ).reshape(length).astype(F32)
    distance = position[:, None] - position[None, :]
    causal = distance >= 0
    decay_mask = jnp.where(
        causal[None],
        jnp.exp(-rates[:, None, None] * jnp.where(causal, distance, 0.0)[None]),
        0.0,
    )
    lead = jnp.exp(-rates[None, :] * (position[:, None] + 1.0))[None, :, :, None]
    tail = jnp.exp(-rates[None, :] * (length - 1.0 - position[:, None]))[None, :, :, None]
    piece_decay = jnp.exp(-rates * length)[None, :, None, None]

    def by_head(values):
        return values.reshape(batch, length, heads, head_dim)

    def flat(values):
        return values.reshape(rows, lanes)

    def product_of(spec, left, right):
        return jnp.einsum(spec, left, right, preferred_element_type=F32)

    pre_qk = dot_nn(normed_in, full_qk)
    query_pre, key_pre = pre_qk[:, :lanes], pre_qk[:, lanes:]
    queries = by_head(jax.nn.silu(query_pre).astype(BF16))
    keys = by_head(jax.nn.silu(key_pre).astype(BF16))
    pre_vg = dot_nn(normed_in, full_vg)
    values = by_head(pre_vg[:, :lanes].astype(BF16))
    gate_lin = pre_vg[:, lanes:]
    keys_tail = (keys * tail).astype(BF16)
    queries_lead = (queries * lead).astype(BF16)
    local_state = product_of("mshd,mshe->mhde", keys_tail, values)
    state_in = earlier_state(local_state, piece_decay, False).astype(BF16)
    scores = product_of("mthd,mshd->mhts", queries, keys)
    weights = (scores * decay_mask[None]).astype(BF16)
    attn_raw = flat(
        product_of("mhts,mshd->mthd", weights, values)
        + product_of("mthd,mhde->mthe", queries_lead, state_in)
    )
    squares = plane_reduce_small(jnp.sum(attn_raw * attn_raw, axis=1))
    attn_gated = (attn_raw * gate_lin).astype(BF16)
    out_sum = plane_reduce(dot_nn(attn_gated, full_out))
    scale_own = lax.rsqrt(squares / width + EPSILON)
    resid_mid = x_own + out_sum * scale_own[:, None]
    scale_mid = rms_scale(resid_mid)
    normed_mid = plane_gather((resid_mid * scale_mid).astype(BF16))

    first_pre = dot_nt(normed_mid, full_first)
    second_pre = dot_nt(normed_mid, full_second)
    product = (first_pre * second_pre).astype(BF16)
    grad_down = scatter_t(jnp.split(dot_tn(product, gy), count, axis=1))
    dproduct = dot_nt(gy, full_down)
    dfirst = (dproduct * second_pre).astype(BF16)
    dsecond = (dproduct * first_pre).astype(BF16)
    dnormed_mid = plane_reduce(dot_nn(dfirst, full_first) + dot_nn(dsecond, full_second))
    grad_first = scatter_t(jnp.split(dot_tn(dfirst, normed_mid), count, axis=1))
    grad_second = scatter_t(jnp.split(dot_tn(dsecond, normed_mid), count, axis=1))
    down_sum = plane_reduce(dot_nn(product, full_down))
    layer_out = own_first(rotate(head_gather((resid_mid + down_sum).astype(BF16)), True), True)

    grad_mid = gy_own + rms_back(resid_mid, scale_mid, dnormed_mid)
    grad_mid_low = grad_mid.astype(BF16)
    inner = jnp.sum(grad_mid_low.astype(F32) * out_sum, axis=-1)
    coefficient = scale_own * scale_own * scale_own / width * inner
    grad_rows = plane_gather(grad_mid_low)
    scalars = plane_gather_small(jnp.stack([scale_own, coefficient], axis=-1)).reshape(rows, 2)
    attn_scale, pull = scalars[:, :1], scalars[:, 1:]
    attn_normed = attn_raw * attn_scale
    gated = (attn_normed * gate_lin).astype(BF16)
    grad_out = scatter_t(jnp.split(dot_tn(gated, grad_rows), count, axis=1))
    dgated = dot_nt(grad_rows, full_out)
    dgate = (dgated * attn_normed).astype(BF16)
    dattn = by_head((attn_scale * (dgated * gate_lin) - pull * attn_raw).astype(BF16))

    passed = product_of("mthd,mthe->mhde", queries_lead, dattn)
    state_later = earlier_state(passed, piece_decay, True).astype(BF16)
    dweights = product_of("mthe,mshe->mhts", dattn, values)
    dscores = (dweights * decay_mask[None]).astype(BF16)
    dqueries = product_of("mhts,mshd->mthd", dscores, keys) + lead * product_of(
        "mthe,mhde->mthd", dattn, state_in
    )
    dkeys = product_of("mhts,mthd->mshd", dscores, queries) + tail * product_of(
        "mshe,mhde->mshd", values, state_later
    )
    dvalues = product_of("mhts,mthe->mshe", weights, dattn) + tail * product_of(
        "mshd,mhde->mshe", keys, state_later
    )
    dquery_pre = (flat(dqueries) * silu_slope(query_pre)).astype(BF16)
    dkey_pre = (flat(dkeys) * silu_slope(key_pre)).astype(BF16)
    d_qk = jnp.concatenate([dquery_pre, dkey_pre], axis=1)
    d_vg = jnp.concatenate([flat(dvalues).astype(BF16), dgate], axis=1)
    grad_qk = scatter_t(jnp.split(dot_tn(normed_in, d_qk), count, axis=0))
    grad_vg = scatter_t(jnp.split(dot_tn(normed_in, d_vg), count, axis=0))
    dnormed_in = plane_reduce(dot_nt(d_qk, full_qk) + dot_nt(d_vg, full_vg))
    input_own = grad_mid + rms_back(x_own, scale_in, dnormed_in)
    input_grad = own_first(
        rotate(head_gather(input_own.astype(BF16)), True), True
    ).astype(F32)

    def back_columns(pair):
        mine, theirs = halves(pair, 0)
        other = swap_u(theirs.astype(BF16)).astype(F32)
        return (
            in_u_order(mine[:, :lanes], other[:, :lanes], 1),
            in_u_order(mine[:, lanes:], other[:, lanes:], 1),
        )

    def back_rows(grad):
        mine, theirs = halves(grad, 1)
        return in_u_order(mine, swap_u(theirs.astype(BF16)).astype(F32), 0)

    grad_query, grad_key = back_columns(grad_qk)
    grad_value, grad_gate = back_columns(grad_vg)
    return (
        layer_out,
        input_grad,
        grad_query,
        grad_key,
        grad_value,
        grad_gate,
        back_rows(grad_out),
        back_rows(grad_first).T,
        back_rows(grad_second).T,
        back_rows(grad_down),
    )


def solution(mesh):
    seq, head = mesh.shape["seq"], mesh.shape["head"]
    fine = Mesh(mesh.devices.reshape(seq // PLANE, PLANE, head), ("t", "u", "head"))
    seq_axes = ("t", "u")
    rows = P(None, seq_axes, None)
    inward = P(seq_axes, "head")
    outward = P("head", seq_axes)
    return jax.shard_map(
        local,
        mesh=fine,
        in_specs=(
            rows,
            inward,
            inward,
            inward,
            inward,
            outward,
            inward,
            inward,
            outward,
            P("head"),
            rows,
        ),
        out_specs=(
            rows,
            rows,
            inward,
            inward,
            inward,
            inward,
            outward,
            inward,
            inward,
            outward,
        ),
        check_vma=False,
    )
```
